256 devices in a mesh: worker: 16 (over x, z_hi, core), fsdp: 16 (over z_lo, y).
Axes of the slice: x: 4, y: 4, z: 8 (z_hi: 2, z_lo: 4; z = z_hi * 4 + z_lo), core: 2. Of those that a mesh axis runs over, the one named last changes fastest.
Arguments:
- inputs: bfloat16 [16, 4096, 8192], P('worker', 'fsdp'), may hold values from -6 to 6
- output_grads: bfloat16 [16, 4096, 1024], P('worker', 'fsdp'), may hold values from -0.25 to 0.25
- local_params: float32 [16, 8192, 1024], P('worker', 'fsdp'), may hold values from -6 to 6
- first_moment: float32 [16, 8192, 1024], P('worker', 'fsdp'), may hold values from -4 to 4
- second_moment: float32 [16, 8192, 1024], P('worker', 'fsdp'), may hold values from 0.01 to 0.1
- global_params: float32 [8192, 1024], P(('fsdp', 'worker')), may hold values from -6 to 6
- momentum: float32 [8192, 1024], P(('fsdp', 'worker')), may hold values from -6 to 6
Outputs:
- new_params: float32 [8192, 1024], P('fsdp')
- new_momentum: float32 [8192, 1024], P(('fsdp', 'worker'))
The draws below stay inside these ranges and needn't reach their ends.
All inputs are finite; a program needn't handle non-finite values.
Results may differ from the reference program's by a relative error of at most 0.0015.
Values may be sent and summed in bfloat16 or wider, within the bound.
A program may use at most 128 MiB of HBM per device.

```python
import math
import jax
import jax.numpy as jnp
from jax import lax

D = 8192
KV = 1024
TOK_DEV = 256
TOKENS = 4096
N_WORKER = 16
N_FSDP = 16


def spiked(array, key, source, target, shards_of, factor):
    def block_of(dim):
        return (jnp.arange(array.shape[dim]) // (array.shape[dim] // shards_of)).reshape((-1,) + (1,) * (array.ndim - 1 - dim))

    one_side = jax.random.permutation(key, shards_of)[block_of(target)]
    second = (block_of(target) + shards_of // 2) % shards_of
    return jnp.where((block_of(source) == one_side) | (block_of(source) == second), factor * array, array)


def steps_of(own_key, extent, pieces, smallest, top_value):
    level, own = 1.0, jax.random.fold_in(own_key, 6)
    for axis_at, parts in pieces:
        draws = jnp.exp(jax.random.uniform(jax.random.fold_in(own, axis_at), (parts,), jnp.float32, smallest / len(pieces), top_value / len(pieces)))
        level = level * jnp.repeat(draws, extent[axis_at] // parts).reshape([-1 if axis == axis_at else 1 for axis in range(len(extent))])
    return level


def noise(stream_key, shape, width, reach, split=(), held_as=jnp.bfloat16):
    factor_of = steps_of(stream_key, shape, split, -0.22, 0.18) if split else 1.0
    entries = jax.random.normal(stream_key, shape, jnp.float32) * width * factor_of
    return jnp.minimum(jnp.maximum(entries, -reach), reach).astype(held_as)


def gaussian_with(rng, dims, width, bound, split, heavy, dtype=jnp.bfloat16):
    entries = width * jax.random.normal(rng, dims, jnp.float32)
    if split:
        entries = entries * steps_of(rng, dims, split, -0.22, 0.18)
    return jnp.clip(spiked(entries, jax.random.fold_in(rng, 3), *heavy), -bound, bound).astype(dtype)


def setup_inputs(seed: int = 0) -> dict:
    splits = jax.random.split(jax.random.key(seed), 8)
    inputs = gaussian_with(splits[0], (N_WORKER, TOKENS, D), 1.0, 6.0, ((0, 16), (1, 16)), (1, 2, 16, 2.0))
    output_grads = noise(splits[1], (N_WORKER, TOKENS, KV), (TOKENS ** -0.5), 0.25, ((0, 16), (1, 16)))
    local_params = noise(splits[2], (N_WORKER, D, KV), 1.0, 6.0, ((0, 16), (1, 16)), jnp.float32)
    first_moment = noise(splits[3], (N_WORKER, D, KV), 0.3, 4.0, ((0, 16), (1, 16)), jnp.float32)
    second_moment = jnp.clip(jnp.exp(math.log(0.1) - 2.3025851 * jax.random.uniform(splits[4], (N_WORKER, D, KV), jnp.float32) ** steps_of(splits[4], (N_WORKER, D, KV), ((0, 16), (1, 16)), -0.2, 0.2)), 0.01, 0.1)
    global_params = noise(splits[5], (D, KV), 1.0, 6.0, ((0, 256),), jnp.float32)
    momentum = noise(splits[6], (D, KV), 0.5, 6.0, ((0, 256),), jnp.float32)
    return dict(inputs=inputs, output_grads=output_grads, local_params=local_params, first_moment=first_moment, second_moment=second_moment, global_params=global_params, momentum=momentum)


beta_first = 0.8
beta_second = 0.9
inner_rate = 0.15
weight_decay = 0.1
adam_epsilon = 1e-08
outer_rate = 0.7
momentum_coef = 0.9
inner_count = 50

def replica_gradient(operands):
    features, cotangents = operands

    def accumulate(source, total):
        begin_row = (source * TOK_DEV).astype(jnp.int32)
        block_in = lax.dynamic_slice_in_dim(features, begin_row, TOK_DEV, 0)
        block_out = lax.dynamic_slice_in_dim(cotangents, begin_row, TOK_DEV, 0)
        partial_term = lax.dot_general(block_in, block_out, (((0,), (0,)), ((), ())), preferred_element_type=jnp.float32)
        rounded = lax.optimization_barrier(partial_term.astype(jnp.bfloat16))
        return total + rounded.astype(jnp.float32)
    start_total = jnp.zeros((D, KV), jnp.float32)
    return lax.fori_loop(0, N_FSDP, accumulate, start_total)

def reference(inputs, output_grads, local_params, first_moment, second_moment, global_params, momentum):
    gradient = lax.map(replica_gradient, (inputs, output_grads))
    moment_one = beta_first * first_moment + (1.0 - beta_first) * gradient
    moment_two = beta_second * second_moment + (1.0 - beta_second) * gradient * gradient
    first_correction = 1.0 - beta_first ** inner_count
    second_correction = 1.0 - beta_second ** inner_count
    ratio = moment_one / first_correction / (jnp.sqrt(moment_two / second_correction) + adam_epsilon)
    stepped = local_params - inner_rate * (ratio + weight_decay * local_params)
    outer_grad = lax.optimization_barrier(jnp.sum(global_params[None] - stepped, axis=0)) / N_WORKER
    new_momentum = momentum_coef * momentum + outer_grad
    new_params = global_params - outer_rate * (outer_grad + momentum_coef * new_momentum)
    return (new_params, new_momentum)
```

```python
import jax
import jax.numpy as jnp
from jax import lax
from jax.experimental import pallas as pl
from jax.experimental.pallas import tpu as pltpu
from jax.sharding import PartitionSpec as P

beta_first = 0.8
beta_second = 0.9
inner_rate = 0.15
weight_decay = 0.1
adam_epsilon = 1e-08
outer_rate = 0.7
momentum_coef = 0.9
inner_count = 50

MESH = pl.DeviceIdType.MESH
NX, NH, NC = 4, 2, 2
NZ, NY = 4, 4
NQ = 4


def kernel(
    x_hbm, g_hbm, lp_hbm, m1_hbm, m2_hbm, gp_hbm, mo_hbm,
    out_hbm, newm_hbm,
    xr, gr, sb, rz, lp, m1, m2, pf, sh, rc, tt, rx, uu, rh, gp, mm, np_, mn,
    xs_s, xs_r, xl, gs_s, gs_r, gl, z_s, z_r, ld, hl, hs_s, hs_r,
    rc_s, rc_r, rx_s, rx_r, rh_s, rh_r, nx_s, nx_r, nc_s, nc_r, od, md,
):
    tok, rows = xr.shape[1] // NY, xr.shape[2]
    wide = gr.shape[2]
    share = gp.shape[1]
    w, f = lax.axis_index("worker"), lax.axis_index("fsdp")
    x, h, c = w // (NH * NC), (w // NC) % NH, w % NC
    z, y = f // NY, f % NY

    def dev(x=x, h=h, c=c, z=z, y=y):
        return {"worker": (x * NH + h) * NC + c, "fsdp": z * NY + y}

    def remote(src, dst, send, recv, to):
        return pltpu.make_async_remote_copy(
            src_ref=src, dst_ref=dst, send_sem=send, recv_sem=recv, device_id=to, device_id_type=MESH
        )

    def cols(q):
        return pl.ds(pl.multiple_of(q * wide, wide), wide)

    order = [3 * (1 - z // 2), (3 * z + 2) % 5, 1 + z % 2, z]
    steps = [1 - 2 * (z // 2), 1 - 2 * (z % 2), 1 - 2 * (z // 2)]
    middle = (z == 1) | (z == 2)

    here = []
    for q in range(NQ):
        here.append(pltpu.make_async_copy(
            g_hbm.at[:, cols(q)], gr.at[q, pl.ds(pl.multiple_of(y * tok, tok), tok)], gl.at[q]))
    for k in range(NZ):
        b = order[k]
        here.append(pltpu.make_async_copy(
            x_hbm.at[:, pl.ds(pl.multiple_of((b * NY + y) * rows, rows), rows)],
            xr.at[b, pl.ds(pl.multiple_of(y * tok, tok), tok)], xl.at[k]))
    loads = [pltpu.make_async_copy(a, v, ld.at[i]) for i, (a, v) in enumerate(
        ((lp_hbm, lp), (m1_hbm, m1), (m2_hbm, m2)))]
    owns = [pltpu.make_async_copy(a, v.at[h], hl.at[i]) for i, (a, v) in enumerate(((gp_hbm, gp), (mo_hbm, mm)))]
    for copy in here + owns + loads:
        copy.start()

    barrier = pltpu.get_barrier_semaphore()
    peers = [dev(y=(y + j) % NY) for j in range(1, NY)]
    peers += [dev(x=(x + j) % NX) for j in range(1, NX)]
    peers += [dev(z=(z + 1) % NZ), dev(z=(z + NZ - 1) % NZ), dev(h=1 - h), dev(c=1 - c)]
    for peer in peers:
        pl.semaphore_signal(barrier, inc=1, device_id=peer, device_id_type=MESH)
    pl.semaphore_wait(barrier, len(peers))

    def x_copy(k, j):
        b, to = order[k], (y + j) % NY
        return remote(
            x_hbm.at[:, pl.ds(pl.multiple_of((b * NY + to) * rows, rows), rows)],
            xr.at[b, pl.ds(pl.multiple_of(y * tok, tok), tok)],
            xs_s.at[k, j - 1], xs_r.at[k, j - 1], dev(y=to))

    def g_copy(q, j):
        return remote(
            g_hbm.at[:, cols(q)], gr.at[q, pl.ds(pl.multiple_of(y * tok, tok), tok)],
            gs_s.at[q, j - 1], gs_r.at[q, j - 1], dev(y=(y + j) % NY))

    near = (1, NY - 1, 2)
    for j in near:
        g_copy(0, j).start()
    for j in near:
        x_copy(0, j).start()
    for q in range(1, NQ):
        for j in near:
            g_copy(q, j).start()
    for k in range(1, NZ):
        for j in near:
            x_copy(k, j).start()
    swaps = [remote(a, v.at[h], hs_s.at[i], hs_r.at[i], dev(h=1 - h)) for i, (a, v) in enumerate(
        ((gp_hbm, gp), (mo_hbm, mm)))]
    for copy in swaps:
        copy.start()

    def product(b, q):
        return lax.dot_general(
            xr[b], gr[q], (((0,), (0,)), ((), ())), preferred_element_type=jnp.float32)

    def z_copy(k, q, b, step):
        slot = (1 - step) // 2
        return remote(sb.at[k, q], rz.at[slot, b, q], z_s.at[k, q], z_r.at[slot, b, q], dev(z=z + step))

    def arrived(slot, b, q):
        remote(rz.at[slot, b, q], rz.at[slot, b, q], z_s.at[0, q], z_r.at[slot, b, q], dev(z=(z + 1) % NZ)).wait_recv()

    for k in range(NZ - 1):
        b, step = order[k], steps[k]
        here[NQ + k].wait()
        for j in near:
            x_copy(k, j).wait_recv()

        def send_piece(q, _, k=k, b=b, step=step):
            if k == 0:
                pltpu.make_async_copy(
                    g_hbm.at[:, cols(q)], gr.at[q, pl.ds(pl.multiple_of(y * tok, tok), tok)], gl.at[q]).wait()
                for j in near:
                    g_copy(q, j).wait_recv()
            part = product(b, q)

            @pl.when(middle)
            def _():
                pf[q] = part
                slot = (1 - step) // 2
                arrived(slot, b, q)
                sb[k, q] = (pf[q] + rz[slot, b, q].astype(jnp.float32)).astype(jnp.bfloat16)

            @pl.when(jnp.logical_not(middle))
            def _():
                sb[k, q] = part.astype(jnp.bfloat16)

            z_copy(k, q, b, step).start()
            return 0

        lax.fori_loop(0, NQ, send_piece, 0)

    here[NQ + NZ - 1].wait()
    for j in near:
        x_copy(NZ - 1, j).wait_recv()

    def own_piece(q, _):
        pf[q] = product(z, q)
        return 0

    lax.fori_loop(0, NQ, own_piece, 0)
    for copy in loads + owns:
        copy.wait()
    for copy in swaps:
        copy.wait_recv()

    first_correction = 1.0 - beta_first**inner_count
    second_correction = 1.0 - beta_second**inner_count

    def rc_copy(q):
        return remote(sh.at[q, 1 - c], rc.at[q], rc_s.at[q], rc_r.at[q], dev(c=1 - c))

    def rx_copy(q, j):
        to = (x + j) % NX
        return remote(tt.at[q, to], rx.at[q, j - 1], rx_s.at[q, j - 1], rx_r.at[q, j - 1], dev(x=to))

    def rh_copy(q):
        return remote(uu.at[q], rh.at[q], rh_s.at[q], rh_r.at[q], dev(h=1 - h))

    def nx_copy(q, j):
        return remote(
            np_.at[q, c, x], np_.at[q, c, x], nx_s.at[q, j - 1], nx_r.at[q, j - 1], dev(x=(x + j) % NX))

    def nx_wait(q, j):
        remote(np_.at[q, c, (x + NX - j) % NX], np_.at[q, c, (x + NX - j) % NX],
               nx_s.at[q, j - 1], nx_r.at[q, j - 1], dev(x=(x + j) % NX)).wait_recv()

    def nc_copy(q):
        return remote(np_.at[q, c], np_.at[q, c], nc_s.at[q], nc_r.at[q], dev(c=1 - c))

    def nc_wait(q):
        remote(np_.at[q, 1 - c], np_.at[q, 1 - c], nc_s.at[q], nc_r.at[q], dev(c=1 - c)).wait_recv()

    def out_copy(q, i):
        return pltpu.make_async_copy(np_.at[q, i], out_hbm.at[:, :, i, :, cols(q)], od.at[q, i])

    def m_copy(q):
        return pltpu.make_async_copy(mn.at[q, h], newm_hbm.at[:, cols(q)], md.at[q])

    def adam(q):
        @pl.when(z > 0)
        def _():
            arrived(0, z, q)
            pf[q] = pf[q] + rz[0, z, q].astype(jnp.float32)

        @pl.when(z < NZ - 1)
        def _():
            arrived(1, z, q)
            pf[q] = pf[q] + rz[1, z, q].astype(jnp.float32)

        def block(i, _):
            at = pl.ds(pl.multiple_of(i * share, share), share)
            grad = pf[q, at]
            moment_one = beta_first * m1[at, cols(q)] + (1.0 - beta_first) * grad
            moment_two = beta_second * m2[at, cols(q)] + (1.0 - beta_second) * grad * grad
            params = lp[at, cols(q)]
            ratio = moment_one / first_correction / (jnp.sqrt(moment_two / second_correction) + adam_epsilon)
            sh[q, i % NC, i // NC] = params - inner_rate * (ratio + weight_decay * params)
            return 0

        lax.fori_loop(0, rows // share, block, 0)
        rc_copy(q).start()

    def to_x(q):
        rc_copy(q).wait_recv()
        total = sh[q, c] + rc[q]
        tt[q] = total.reshape(tt.shape[1:])
        for j in near:
            rx_copy(q, j).start()

    def to_h(q):
        for j in near:
            rx_copy(q, j).wait_recv()
        uu[q] = tt[q, x] + rx[q, 0] + rx[q, 1] + rx[q, 2]
        rh_copy(q).start()

    def update(q):
        rh_copy(q).wait_recv()
        mean = (uu[q] + rh[q]) * (1.0 / (NX * NH * NC))
        anchor = gp[:, :, cols(q)]
        outer_grad = anchor - mean
        fresh = momentum_coef * mm[:, :, cols(q)] + outer_grad
        mn[q] = fresh
        np_[q, c, x] = anchor - outer_rate * (outer_grad + momentum_coef * fresh)
        for j in near:
            nx_copy(q, j).start()
        m_copy(q).start()

    def to_core(q):
        for j in near:
            nx_wait(q, j)
        nc_copy(q).start()
        out_copy(q, c).start()

    def finish(q):
        nc_wait(q)
        out_copy(q, 1 - c).start()

    def turn(t, _):
        for lag, stage in ((0, adam), (0, to_x), (1, to_h), (2, update), (3, to_core), (4, finish)):
            @pl.when((t >= lag) & (t < NQ + lag))
            def _(lag=lag, stage=stage):
                stage(t - lag)
        return 0

    lax.fori_loop(0, NQ + 4, turn, 0)

    def drain(q, _):
        for j in near:
            g_copy(q, j).wait_send()
            rx_copy(q, j).wait_send()
            nx_copy(q, j).wait_send()
        for k in range(NZ - 1):
            z_copy(k, q, order[k], steps[k]).wait_send()
        rc_copy(q).wait_send()
        rh_copy(q).wait_send()
        nc_copy(q).wait_send()
        out_copy(q, c).wait()
        out_copy(q, 1 - c).wait()
        m_copy(q).wait()
        return 0

    lax.fori_loop(0, NQ, drain, 0)
    for k in range(NZ):
        for j in near:
            x_copy(k, j).wait_send()
    for copy in swaps:
        copy.wait_send()


def shards(
    inputs, output_grads, local_params, first_moment, second_moment, global_params, momentum
):
    tok, width = inputs.shape[1], output_grads.shape[2]
    rows, share = local_params.shape[1], global_params.shape[0]
    wide = width // NQ
    f32, bf16 = jnp.float32, jnp.bfloat16
    dma = pltpu.SemaphoreType.DMA
    ins = (inputs[0], output_grads[0], local_params[0], first_moment[0], second_moment[0], global_params, momentum)
    own = (NX, NH, share, wide)
    new_params, new_momentum = pl.pallas_call(
        kernel,
        out_shape=(
            jax.ShapeDtypeStruct((NX, NH, NC, share, width), f32),
            jax.ShapeDtypeStruct((share, width), f32),
        ),
        in_specs=[pl.BlockSpec(memory_space=pl.ANY)] * len(ins),
        out_specs=(pl.BlockSpec(memory_space=pl.ANY),) * 2,
        scratch_shapes=[
            pltpu.VMEM((NZ, NY * tok, rows), bf16),
            pltpu.VMEM((NQ, NY * tok, wide), bf16),
            pltpu.VMEM((NZ - 1, NQ, rows, wide), bf16),
            pltpu.VMEM((2, NZ, NQ, rows, wide), bf16),
            pltpu.VMEM((rows, width), f32),
            pltpu.VMEM((rows, width), f32),
            pltpu.VMEM((rows, width), f32),
            pltpu.VMEM((NQ, rows, wide), f32),
            pltpu.VMEM((NQ, NC, NX * NH, share, wide), f32),
            pltpu.VMEM((NQ, NX * NH, share, wide), f32),
            pltpu.VMEM((NQ,) + own, f32),
            pltpu.VMEM((NQ, NX - 1, NH, share, wide), f32),
            pltpu.VMEM((NQ, NH, share, wide), f32),
            pltpu.VMEM((NQ, NH, share, wide), f32),
            pltpu.VMEM((NH, share, width), f32),
            pltpu.VMEM((NH, share, width), f32),
            pltpu.VMEM((NQ, NC) + own, f32),
            pltpu.VMEM((NQ, NH, share, wide), f32),
            dma((NZ, NY - 1)), dma((NZ, NY - 1)), dma((NZ,)),
            dma((NQ, NY - 1)), dma((NQ, NY - 1)), dma((NQ,)),
            dma((NZ - 1, NQ)), dma((2, NZ, NQ)), dma((3,)), dma((2,)), dma((2,)), dma((2,)),
            dma((NQ,)), dma((NQ,)), dma((NQ, NX - 1)), dma((NQ, NX - 1)), dma((NQ,)), dma((NQ,)),
            dma((NQ, NX - 1)), dma((NQ, NX - 1)), dma((NQ,)), dma((NQ,)), dma((NQ, NC)), dma((NQ,)),
        ],
        compiler_params=pltpu.CompilerParams(
            collective_id=0, has_side_effects=True, vmem_limit_bytes=56 << 20
        ),
    )(*ins)
    return (new_params.reshape(rows, width), new_momentum)


def solution(mesh):
    return jax.shard_map(
        shards,
        mesh=mesh,
        in_specs=(
            P("worker", "fsdp", None),
            P("worker", "fsdp", None),
            P("worker", "fsdp", None),
            P("worker", "fsdp", None),
            P("worker", "fsdp", None),
            P(("fsdp", "worker"), None),
            P(("fsdp", "worker"), None),
        ),
        out_specs=(P("fsdp", None), P(("fsdp", "worker"), None)),
        check_vma=False,
    )
```

```python
import jax
import jax.numpy as jnp
from jax import lax
from jax.experimental import pallas as pl
from jax.experimental.pallas import tpu as pltpu
from jax.sharding import PartitionSpec as P

beta_first = 0.8
beta_second = 0.9
inner_rate = 0.15
weight_decay = 0.1
adam_epsilon = 1e-08
outer_rate = 0.7
momentum_coef = 0.9
inner_count = 50

MESH = pl.DeviceIdType.MESH
NX, NH, NC = 4, 2, 2
NZ, NY = 4, 4
NQ = 4


def kernel(
    x_hbm, g_hbm, lp_hbm, m1_hbm, m2_hbm, gp_hbm, mo_hbm,
    out_hbm, newm_hbm,
    xv, xr, gr, sb, rz, lp, m1, m2, pf, sh, rc, tt, rx, uu, rh, gp, mm, np_, mn,
    xw, xs_s, xs_r, xl, gs_s, gs_r, gl, z_s, z_r, ld, hl, hs_s, hs_r,
    rc_s, rc_r, rx_s, rx_r, rh_s, rh_r, nx_s, nx_r, nc_s, nc_r, od, md,
):
    tok, rows = xr.shape[1] // NY, xr.shape[2]
    wide = gr.shape[2]
    share = gp.shape[1]
    w, f = lax.axis_index("worker"), lax.axis_index("fsdp")
    x, h, c = w // (NH * NC), (w // NC) % NH, w % NC
    z, y = f // NY, f % NY

    def dev(x=x, h=h, c=c, z=z, y=y):
        return {"worker": (x * NH + h) * NC + c, "fsdp": z * NY + y}

    def remote(src, dst, send, recv, to):
        return pltpu.make_async_remote_copy(
            src_ref=src, dst_ref=dst, send_sem=send, recv_sem=recv, device_id=to, device_id_type=MESH
        )

    def cols(q):
        return pl.ds(pl.multiple_of(q * wide, wide), wide)

    order = [3 * (1 - z // 2), (3 * z + 2) % 5, 1 + z % 2, z]
    steps = [1 - 2 * (z // 2), 1 - 2 * (z % 2), 1 - 2 * (z // 2)]
    middle = (z == 1) | (z == 2)

    brought = [
        pltpu.make_async_copy(
            x_hbm.at[:, pl.ds(pl.multiple_of(order[k] * NY * rows, NY * rows), NY * rows)], xv.at[k], xw.at[k])
        for k in range(NZ)
    ]
    for copy in brought:
        copy.start()
    here = []
    for q in range(NQ):
        here.append(pltpu.make_async_copy(
            g_hbm.at[:, cols(q)], gr.at[q, pl.ds(pl.multiple_of(y * tok, tok), tok)], gl.at[q]))
    for k in range(NZ):
        b = order[k]
        here.append(pltpu.make_async_copy(
            x_hbm.at[:, pl.ds(pl.multiple_of((b * NY + y) * rows, rows), rows)],
            xr.at[b, pl.ds(pl.multiple_of(y * tok, tok), tok)], xl.at[k]))
    loads = [pltpu.make_async_copy(a, v, ld.at[i]) for i, (a, v) in enumerate(
        ((lp_hbm, lp), (m1_hbm, m1), (m2_hbm, m2)))]
    owns = [pltpu.make_async_copy(a, v.at[h], hl.at[i]) for i, (a, v) in enumerate(((gp_hbm, gp), (mo_hbm, mm)))]
    for copy in here + owns + loads:
        copy.start()

    barrier = pltpu.get_barrier_semaphore()
    peers = [dev(y=(y + j) % NY) for j in range(1, NY)]
    peers += [dev(x=(x + j) % NX) for j in range(1, NX)]
    peers += [dev(z=(z + 1) % NZ), dev(z=(z + NZ - 1) % NZ), dev(h=1 - h), dev(c=1 - c)]
    for peer in peers:
        pl.semaphore_signal(barrier, inc=1, device_id=peer, device_id_type=MESH)
    pl.semaphore_wait(barrier, len(peers))

    def x_copy(k, j):
        b, to = order[k], (y + j) % NY
        return remote(
            xv.at[k, :, pl.ds(pl.multiple_of(to * rows, rows), rows)],
            xr.at[b, pl.ds(pl.multiple_of(y * tok, tok), tok)],
            xs_s.at[k, j - 1], xs_r.at[k, j - 1], dev(y=to))

    def g_copy(q, j):
        return remote(
            g_hbm.at[:, cols(q)], gr.at[q, pl.ds(pl.multiple_of(y * tok, tok), tok)],
            gs_s.at[q, j - 1], gs_r.at[q, j - 1], dev(y=(y + j) % NY))

    near = (1, NY - 1, 2)
    for j in near:
        g_copy(0, j).start()
    brought[0].wait()
    for j in near:
        x_copy(0, j).start()
    for q in range(1, NQ):
        for j in near:
            g_copy(q, j).start()
    for k in range(1, NZ):
        brought[k].wait()
        for j in near:
            x_copy(k, j).start()
    swaps = [remote(a, v.at[h], hs_s.at[i], hs_r.at[i], dev(h=1 - h)) for i, (a, v) in enumerate(
        ((gp_hbm, gp), (mo_hbm, mm)))]
    for copy in swaps:
        copy.start()

    def product(b, q):
        return lax.dot_general(
            xr[b], gr[q], (((0,), (0,)), ((), ())), preferred_element_type=jnp.float32)

    def z_copy(k, q, b, step):
        slot = (1 - step) // 2
        return remote(sb.at[k, q], rz.at[slot, b, q], z_s.at[k, q], z_r.at[slot, b, q], dev(z=z + step))

    def arrived(slot, b, q):
        remote(rz.at[slot, b, q], rz.at[slot, b, q], z_s.at[0, q], z_r.at[slot, b, q], dev(z=(z + 1) % NZ)).wait_recv()

    for k in range(NZ - 1):
        b, step = order[k], steps[k]
        here[NQ + k].wait()
        for j in near:
            x_copy(k, j).wait_recv()

        def send_piece(q, _, k=k, b=b, step=step):
            if k == 0:
                pltpu.make_async_copy(
                    g_hbm.at[:, cols(q)], gr.at[q, pl.ds(pl.multiple_of(y * tok, tok), tok)], gl.at[q]).wait()
                for j in near:
                    g_copy(q, j).wait_recv()
            part = product(b, q)

            @pl.when(middle)
            def _():
                pf[q] = part
                slot = (1 - step) // 2
                arrived(slot, b, q)
                sb[k, q] = (pf[q] + rz[slot, b, q].astype(jnp.float32)).astype(jnp.bfloat16)

            @pl.when(jnp.logical_not(middle))
            def _():
                sb[k, q] = part.astype(jnp.bfloat16)

            z_copy(k, q, b, step).start()
            return 0

        lax.fori_loop(0, NQ, send_piece, 0)

    here[NQ + NZ - 1].wait()
    for j in near:
        x_copy(NZ - 1, j).wait_recv()

    def own_piece(q, _):
        pf[q] = product(z, q)
        return 0

    lax.fori_loop(0, NQ, own_piece, 0)
    for copy in loads + owns:
        copy.wait()
    for copy in swaps:
        copy.wait_recv()

    first_correction = 1.0 - beta_first**inner_count
    second_correction = 1.0 - beta_second**inner_count

    def rc_copy(q):
        return remote(sh.at[q, 1 - c], rc.at[q], rc_s.at[q], rc_r.at[q], dev(c=1 - c))

    def rx_copy(q, j):
        to = (x + j) % NX
        return remote(tt.at[q, to], rx.at[q, j - 1], rx_s.at[q, j - 1], rx_r.at[q, j - 1], dev(x=to))

    def rh_copy(q):
        return remote(uu.at[q], rh.at[q], rh_s.at[q], rh_r.at[q], dev(h=1 - h))

    def nx_copy(q, j):
        return remote(
            np_.at[q, c, x], np_.at[q, c, x], nx_s.at[q, j - 1], nx_r.at[q, j - 1], dev(x=(x + j) % NX))

    def nx_wait(q, j):
        remote(np_.at[q, c, (x + NX - j) % NX], np_.at[q, c, (x + NX - j) % NX],
               nx_s.at[q, j - 1], nx_r.at[q, j - 1], dev(x=(x + j) % NX)).wait_recv()

    def nc_copy(q):
        return remote(np_.at[q, c], np_.at[q, c], nc_s.at[q], nc_r.at[q], dev(c=1 - c))

    def nc_wait(q):
        remote(np_.at[q, 1 - c], np_.at[q, 1 - c], nc_s.at[q], nc_r.at[q], dev(c=1 - c)).wait_recv()

    def out_copy(q, i):
        return pltpu.make_async_copy(np_.at[q, i], out_hbm.at[:, :, i, :, cols(q)], od.at[q, i])

    def m_copy(q):
        return pltpu.make_async_copy(mn.at[q, h], newm_hbm.at[:, cols(q)], md.at[q])

    def adam(q):
        @pl.when(z > 0)
        def _():
            arrived(0, z, q)
            pf[q] = pf[q] + rz[0, z, q].astype(jnp.float32)

        @pl.when(z < NZ - 1)
        def _():
            arrived(1, z, q)
            pf[q] = pf[q] + rz[1, z, q].astype(jnp.float32)

        def block(i, _):
            at = pl.ds(pl.multiple_of(i * share, share), share)
            grad = pf[q, at]
            moment_one = beta_first * m1[at, cols(q)] + (1.0 - beta_first) * grad
            moment_two = beta_second * m2[at, cols(q)] + (1.0 - beta_second) * grad * grad
            params = lp[at, cols(q)]
            ratio = moment_one / first_correction / (jnp.sqrt(moment_two / second_correction) + adam_epsilon)
            sh[q, i % NC, i // NC] = params - inner_rate * (ratio + weight_decay * params)
            return 0

        lax.fori_loop(0, rows // share, block, 0)
        rc_copy(q).start()

    def to_x(q):
        rc_copy(q).wait_recv()
        total = sh[q, c] + rc[q]
        tt[q] = total.reshape(tt.shape[1:])
        for j in near:
            rx_copy(q, j).start()

    def to_h(q):
        for j in near:
            rx_copy(q, j).wait_recv()
        uu[q] = tt[q, x] + rx[q, 0] + rx[q, 1] + rx[q, 2]
        rh_copy(q).start()

    def update(q):
        rh_copy(q).wait_recv()
        mean = (uu[q] + rh[q]) * (1.0 / (NX * NH * NC))
        anchor = gp[:, :, cols(q)]
        outer_grad = anchor - mean
        fresh = momentum_coef * mm[:, :, cols(q)] + outer_grad
        mn[q] = fresh
        np_[q, c, x] = anchor - outer_rate * (outer_grad + momentum_coef * fresh)
        for j in near:
            nx_copy(q, j).start()
        m_copy(q).start()

    def to_core(q):
        for j in near:
            nx_wait(q, j)
        nc_copy(q).start()
        out_copy(q, c).start()

    def finish(q):
        nc_wait(q)
        out_copy(q, 1 - c).start()

    def turn(t, _):
        for lag, stage in ((0, adam), (1, to_x), (2, to_h), (3, update), (4, to_core), (5, finish)):
            @pl.when((t >= lag) & (t < NQ + lag))
            def _(lag=lag, stage=stage):
                stage(t - lag)
        return 0

    lax.fori_loop(0, NQ + 5, turn, 0)

    def drain(q, _):
        for j in near:
            g_copy(q, j).wait_send()
            rx_copy(q, j).wait_send()
            nx_copy(q, j).wait_send()
        for k in range(NZ - 1):
            z_copy(k, q, order[k], steps[k]).wait_send()
        rc_copy(q).wait_send()
        rh_copy(q).wait_send()
        nc_copy(q).wait_send()
        out_copy(q, c).wait()
        out_copy(q, 1 - c).wait()
        m_copy(q).wait()
        return 0

    lax.fori_loop(0, NQ, drain, 0)
    for k in range(NZ):
        for j in near:
            x_copy(k, j).wait_send()
    for copy in swaps:
        copy.wait_send()


def shards(
    inputs, output_grads, local_params, first_moment, second_moment, global_params, momentum
):
    tok, width = inputs.shape[1], output_grads.shape[2]
    rows, share = local_params.shape[1], global_params.shape[0]
    wide = width // NQ
    f32, bf16 = jnp.float32, jnp.bfloat16
    dma = pltpu.SemaphoreType.DMA
    ins = (inputs[0], output_grads[0], local_params[0], first_moment[0], second_moment[0], global_params, momentum)
    own = (NX, NH, share, wide)
    new_params, new_momentum = pl.pallas_call(
        kernel,
        out_shape=(
            jax.ShapeDtypeStruct((NX, NH, NC, share, width), f32),
            jax.ShapeDtypeStruct((share, width), f32),
        ),
        in_specs=[pl.BlockSpec(memory_space=pl.ANY)] * len(ins),
        out_specs=(pl.BlockSpec(memory_space=pl.ANY),) * 2,
        scratch_shapes=[
            pltpu.VMEM((NZ, tok, NY * rows), bf16),
            pltpu.VMEM((NZ, NY * tok, rows), bf16),
            pltpu.VMEM((NQ, NY * tok, wide), bf16),
            pltpu.VMEM((NZ - 1, NQ, rows, wide), bf16),
            pltpu.VMEM((2, NZ, NQ, rows, wide), bf16),
            pltpu.VMEM((rows, width), f32),
            pltpu.VMEM((rows, width), f32),
            pltpu.VMEM((rows, width), f32),
            pltpu.VMEM((NQ, rows, wide), f32),
            pltpu.VMEM((NQ, NC, NX * NH, share, wide), f32),
            pltpu.VMEM((NQ, NX * NH, share, wide), f32),
            pltpu.VMEM((NQ,) + own, f32),
            pltpu.VMEM((NQ, NX - 1, NH, share, wide), f32),
            pltpu.VMEM((NQ, NH, share, wide), f32),
            pltpu.VMEM((NQ, NH, share, wide), f32),
            pltpu.VMEM((NH, share, width), f32),
            pltpu.VMEM((NH, share, width), f32),
            pltpu.VMEM((NQ, NC) + own, f32),
            pltpu.VMEM((NQ, NH, share, wide), f32),
            dma((NZ,)), dma((NZ, NY - 1)), dma((NZ, NY - 1)), dma((NZ,)),
            dma((NQ, NY - 1)), dma((NQ, NY - 1)), dma((NQ,)),
            dma((NZ - 1, NQ)), dma((2, NZ, NQ)), dma((3,)), dma((2,)), dma((2,)), dma((2,)),
            dma((NQ,)), dma((NQ,)), dma((NQ, NX - 1)), dma((NQ, NX - 1)), dma((NQ,)), dma((NQ,)),
            dma((NQ, NX - 1)), dma((NQ, NX - 1)), dma((NQ,)), dma((NQ,)), dma((NQ, NC)), dma((NQ,)),
        ],
        compiler_params=pltpu.CompilerParams(
            collective_id=0, has_side_effects=True, vmem_limit_bytes=56 << 20
        ),
    )(*ins)
    return (new_params.reshape(rows, width), new_momentum)


def solution(mesh):
    return jax.shard_map(
        shards,
        mesh=mesh,
        in_specs=(
            P("worker", "fsdp", None),
            P("worker", "fsdp", None),
            P("worker", "fsdp", None),
            P("worker", "fsdp", None),
            P("worker", "fsdp", None),
            P(("fsdp", "worker"), None),
            P(("fsdp", "worker"), None),
        ),
        out_specs=(P("fsdp", None), P(("fsdp", "worker"), None)),
        check_vma=False,
    )
```
